512 devices in a mesh: row: 16 (over z_hi, y), col: 32 (over z_lo, x, core).
Axes of the slice: x: 4, y: 8, z: 8 (z_hi: 2, z_lo: 4; z = z_hi * 4 + z_lo), core: 2. Of those that a mesh axis runs over, the one named last changes fastest.
Arguments:
- amplitudes: bfloat16 [16384, 16384], P('row', 'col'), may hold values from -6 to 6
- aux_left: bfloat16 [16384, 1024], P('col', 'row'), may hold values from -0.046875 to 0.046875
- aux_right: bfloat16 [16384, 1024], P('col', 'row'), may hold values from -0.1875 to 0.1875
- occupied_map: int32 [16384], replicated, may hold values from 0 to 63
- virtual_map: int32 [16384], replicated, may hold values from 0 to 255
- occupied_energy: float32 [64], replicated, may hold values from -3 to -0.5
- virtual_energy: float32 [256], replicated, may hold values from 0.5 to 4
Outputs:
- residual_term: float32 [16384, 16384], P('row', 'col')
The draws below stay inside these ranges and needn't reach their ends.
All inputs are finite; a program needn't handle non-finite values.
Results may differ from the reference program's by a relative error of at most 0.0029.
Values may be sent and summed in bfloat16 or wider, within the bound.
No kernel may reach another device: no remote copies, remote signals or barrier semaphores. Data moves between devices by JAX's collectives and lax.ppermute only.
A program may use at most 64 MiB of HBM per device.

```python
import jax
import jax.numpy as jnp
from jax import lax

NO = 64
NV = 256
AUX = 1024
NT = 16384


def with_ends(array, own_key, smallest, high):
    longest = array.shape.index(max(array.shape))
    spots = []
    for shift in (0, 1):
        where = [jax.random.randint(jax.random.fold_in(own_key, axis), (), 0, length) for axis, length in enumerate(array.shape)]
        where[longest] = (where[longest] + shift) % array.shape[longest]
        spots.append(tuple(where))
    return array.at[spots[0]].set(smallest).at[spots[1]].set(high)


def level_of(own_key, dims, pieces, least, high):
    factor_of = 1.0
    for position, shards_of in pieces:
        heights = jax.random.uniform(jax.random.fold_in(jax.random.fold_in(own_key, 6), position), (shards_of,), jnp.float32, least / len(pieces), high / len(pieces))
        factor_of = factor_of * jnp.repeat(jnp.exp(heights), dims[position] // shards_of).reshape((-1,) + (1,) * (len(dims) - 1 - position))
    return factor_of


def gaussian(own_key, dims, deviation, most, shards=(), held_as=jnp.bfloat16):
    gain = level_of(own_key, dims, shards, -0.22, 0.18) if shards else 1.0
    result = jax.random.normal(own_key, dims, jnp.float32) * deviation * gain
    return jnp.minimum(jnp.maximum(result, -most), most).astype(held_as)


def setup_inputs(seed: int = 0) -> dict:
    key_of = jax.random.split(jax.random.key(seed), 8)
    return {
        "amplitudes": gaussian(key_of[0], (NT, NT), 1.0, 6.0, ((0, 16), (1, 32))),
        "aux_left": gaussian(key_of[1], (NT, AUX), NT ** -0.5, 0.046875, ((0, 32), (1, 16))),
        "aux_right": gaussian(key_of[2], (NT, AUX), AUX ** -0.5, 0.1875, ((0, 32), (1, 16))),
        "occupied_map": with_ends(jax.random.randint(key_of[3], (NT,), 0, NO), jax.random.fold_in(key_of[3], 1), 0, NO - 1).astype(jnp.int32),
        "virtual_map": with_ends(jax.random.randint(key_of[4], (NT,), 0, NV), jax.random.fold_in(key_of[4], 1), 0, NV - 1).astype(jnp.int32),
        "occupied_energy": jnp.clip(jax.random.uniform(key_of[5], (NO,), jnp.float32, -3.0, -0.5), -3.0, -0.5),
        "virtual_energy": jnp.clip(jax.random.uniform(key_of[6], (NV,), jnp.float32, 0.5, 4.0), 0.5, 4.0),
    }


def reference(amplitudes, aux_left, aux_right, occupied_map, virtual_map, occupied_energy, virtual_energy):
    fitted = jnp.dot(amplitudes, aux_left, preferred_element_type=jnp.float32).astype(jnp.bfloat16)
    mixed = lax.dot_general(fitted, aux_right, (((1,), (1,)), ((), ())), preferred_element_type=jnp.float32)
    gap = virtual_energy[virtual_map] - occupied_energy[occupied_map]
    denominator = gap[:, None] + gap[None, :]
    return (mixed + mixed.T) / denominator
```

```python
import itertools

import jax
import jax.numpy as jnp
from jax import lax
from jax.sharding import Mesh
from jax.sharding import PartitionSpec as P

ROW = ("zh", "y")
COL = ("zl", "x")
AUX_COL = ("x", "zl")
ALL = ("zh", "y", "zl", "x", "core")
SIZES = (2, 8, 4, 4, 2)
SWAP = [(0, 1), (1, 0)]
X_SCALE = 128.0
Z_SCALE = 32.0


def device_of(zh, y, zl, x, core):
    return (((zh * 8 + y) * 4 + zl) * 4 + x) * 2 + core


def chips(flip, move):
    pairs = []
    for zh, y, zl, x, core in itertools.product(*(range(n) for n in SIZES)):
        there = move(zh, y, zl, x)
        pairs.append((device_of(zh, y, zl, x, core), device_of(*there, core ^ flip)))
    return pairs


def to_column(zh, y, zl, x):
    part, block = x * 4 + zl, zh * 8 + y
    return part // 8, part % 8, block // 4, block % 4


def to_row(zh, y, zl, x):
    part, block = zh * 8 + y, zl * 4 + x
    return block // 8, block % 8, part % 4, part // 4


def spread(chunk, axes, count):
    return lax.all_to_all(jnp.broadcast_to(chunk[None], (count,) + chunk.shape), axes, 0, 0)


def lookup(positions, energy_table):
    matches = positions[:, None] == jnp.arange(energy_table.shape[0], dtype=jnp.int32)[None, :]
    return jnp.sum(jnp.where(matches, energy_table[None, :], 0.0), axis=1)


def pair_gap(occupied_map, virtual_map, occupied_energy, virtual_energy, offset, length):
    occupied_part = lax.dynamic_slice_in_dim(occupied_map, offset, length, 0)
    virtual_part = lax.dynamic_slice_in_dim(virtual_map, offset, length, 0)
    return lookup(virtual_part, virtual_energy) - lookup(occupied_part, occupied_energy)


def contract(left, right):
    return lax.dot_general(
        left, right, (((0,), (0,)), ((), ())), preferred_element_type=jnp.float32
    )


def per_device(
    amplitudes, aux_left, aux_right, occupied_map, virtual_map, occupied_energy, virtual_energy
):
    rows, cols = amplitudes.shape
    core = lax.axis_index("core")
    first = core == 0
    row_block = lax.axis_index(ROW)
    col_block = lax.axis_index(COL + ("core",))

    left = aux_left.T.reshape(2, 32, cols)
    kept = lax.dynamic_index_in_dim(left, core, 0, keepdims=False)
    given = lax.dynamic_index_in_dim(left, 1 - core, 0, keepdims=False)
    taken = lax.ppermute(given, "core", SWAP)
    left_chunk = jnp.concatenate([kept, taken], axis=1)
    left_full = spread(left_chunk, ROW, 16).reshape(512, 2 * cols)
    other_amplitudes = lax.ppermute(amplitudes, "core", SWAP)
    wide = jnp.concatenate([amplitudes, other_amplitudes], axis=1)

    right = aux_right.T
    right_moved = lax.ppermute(right, ALL, chips(0, to_row))
    right_rows = spread(right_moved, AUX_COL, 16).reshape(1024, cols)
    right_rows_other = lax.ppermute(right_rows, "core", SWAP)
    right_rows = jnp.concatenate(
        [
            jnp.where(first, right_rows, right_rows_other),
            jnp.where(first, right_rows_other, right_rows),
        ],
        axis=1,
    )
    right_cols = spread(right, ROW, 16).reshape(16, 2, 32, cols)
    right_kept = lax.dynamic_index_in_dim(right_cols, core, 1, keepdims=False).reshape(512, cols)
    right_other = lax.dynamic_index_in_dim(right_cols, 1 - core, 1, keepdims=False).reshape(
        512, cols
    )

    partial = lax.dot_general(
        left_full, wide, (((1,), (1,)), ((), ())), preferred_element_type=jnp.float32
    )
    sent = (partial * X_SCALE).astype(jnp.float16).reshape(4, 128, rows)
    summed = jnp.sum(lax.all_to_all(sent, "x", 0, 0).astype(jnp.float32), axis=0)
    sent = (summed * (Z_SCALE / X_SCALE)).astype(jnp.float16).reshape(4, 32, rows)
    summed = jnp.sum(lax.all_to_all(sent, "zl", 0, 0).astype(jnp.float32), axis=0)
    fitted = (summed * (1.0 / Z_SCALE)).astype(jnp.bfloat16)

    fitted_kept = lax.dynamic_slice_in_dim(fitted, core * cols, cols, 1)
    fitted_given = lax.dynamic_slice_in_dim(fitted, (1 - core) * cols, cols, 1)
    same = lax.ppermute(fitted_kept, ALL, chips(0, to_column))
    cross = lax.ppermute(fitted_given, ALL, chips(1, to_column))
    mirror_chunk = jnp.concatenate(
        [jnp.where(first, same, cross), jnp.where(first, cross, same)], axis=0
    )
    mirror = spread(mirror_chunk, ROW, 16).reshape(1024, cols)
    fitted_half = spread(fitted, AUX_COL, 16).reshape(512, rows)
    fitted_other = lax.ppermute(fitted_half, "core", SWAP)

    mixed = contract(fitted_half, right_kept) + contract(fitted_other, right_other)
    mirrored = contract(right_rows, mirror)
    row_gap = pair_gap(
        occupied_map, virtual_map, occupied_energy, virtual_energy, row_block * rows, rows
    )
    col_gap = pair_gap(
        occupied_map, virtual_map, occupied_energy, virtual_energy, col_block * cols, cols
    )
    return (mixed + mirrored) / (row_gap[:, None] + col_gap[None, :])


def solution(mesh):
    fine = Mesh(mesh.devices.reshape(SIZES), ALL)
    by_block = P(ROW, COL + ("core",))
    by_aux = P(COL + ("core",), ROW)
    return jax.shard_map(
        per_device,
        mesh=fine,
        in_specs=(by_block, by_aux, by_aux, P(), P(), P(), P()),
        out_specs=by_block,
        check_vma=False,
    )
```

```python
import itertools

import jax
import jax.numpy as jnp
from jax import lax
from jax.sharding import Mesh
from jax.sharding import PartitionSpec as P

ROW = ("zh", "y")
COL = ("zl", "x")
AUX_COL = ("x", "zl")
ALL = ("zh", "y", "zl", "x", "core")
SIZES = (2, 8, 4, 4, 2)
SWAP = [(0, 1), (1, 0)]
LEFT_SCALE = 2.0**20
RIGHT_SCALE = 2.0**18
FIT_SCALE = 8.0
X_SCALE = 128.0
Z_SCALE = 32.0


def device_of(zh, y, zl, x, core):
    return (((zh * 8 + y) * 4 + zl) * 4 + x) * 2 + core


def chips(flip, move, far=0):
    pairs = []
    for zh, y, zl, x, core in itertools.product(*(range(n) for n in SIZES)):
        to_zh, *rest = move(zh, y, zl, x)
        pairs.append((device_of(zh, y, zl, x, core), device_of(to_zh ^ far, *rest, core ^ flip)))
    return pairs


def to_column(zh, y, zl, x):
    slot, block = x * 4 + zl, zh * 8 + y
    return zh ^ (slot & 1), slot >> 1, block // 4, block % 4


def to_row(zh, y, zl, x):
    block = zl * 4 + x
    to_zh, to_y = block // 8, block % 8
    slot = y * 2 + (zh ^ to_zh)
    return to_zh, to_y, slot % 4, slot // 4


def spread(chunk, axes, count):
    return lax.all_to_all(jnp.broadcast_to(chunk[None], (count,) + chunk.shape), axes, 0, 0)


def restore(values, scale):
    return (values.astype(jnp.float32) * (1.0 / scale)).astype(jnp.bfloat16)


def lookup(positions, energy_table):
    matches = positions[:, None] == jnp.arange(energy_table.shape[0], dtype=jnp.int32)[None, :]
    return jnp.sum(jnp.where(matches, energy_table[None, :], 0.0), axis=1)


def pair_gap(occupied_map, virtual_map, occupied_energy, virtual_energy, offset, length):
    occupied_part = lax.dynamic_slice_in_dim(occupied_map, offset, length, 0)
    virtual_part = lax.dynamic_slice_in_dim(virtual_map, offset, length, 0)
    return lookup(virtual_part, virtual_energy) - lookup(occupied_part, occupied_energy)


def contract(left, right):
    return lax.dot_general(
        left, right, (((0,), (0,)), ((), ())), preferred_element_type=jnp.float32
    )


def per_device(
    amplitudes, aux_left, aux_right, occupied_map, virtual_map, occupied_energy, virtual_energy
):
    rows, cols = amplitudes.shape
    core = lax.axis_index("core")
    first = core == 0
    row_block = lax.axis_index(ROW)
    col_block = lax.axis_index(COL + ("core",))

    left = (aux_left.T.astype(jnp.float32) * LEFT_SCALE).astype(jnp.float16).reshape(2, 32, cols)
    kept = lax.dynamic_index_in_dim(left, core, 0, keepdims=False)
    given = lax.dynamic_index_in_dim(left, 1 - core, 0, keepdims=False)
    taken = lax.ppermute(given, "core", SWAP)
    right = (aux_right.T.astype(jnp.float32) * RIGHT_SCALE).astype(jnp.float16)
    chunk = jnp.concatenate([kept, taken, right], axis=0)
    far_chunk = lax.ppermute(chunk, "zh", SWAP)
    factors = lax.all_gather(jnp.stack([chunk, far_chunk]), "y", axis=0, tiled=True)
    left_kept = restore(factors[:, :32], LEFT_SCALE).reshape(512, cols)
    left_taken = restore(factors[:, 32:64], LEFT_SCALE).reshape(512, cols)
    right_cols = factors[:, 64:].reshape(16, 2, 32, cols)
    right_kept = lax.dynamic_index_in_dim(right_cols, core, 1, keepdims=False)
    right_kept = restore(right_kept, RIGHT_SCALE).reshape(512, cols)
    right_other = lax.dynamic_index_in_dim(right_cols, 1 - core, 1, keepdims=False)
    right_other = restore(right_other, RIGHT_SCALE).reshape(512, cols)
    other_amplitudes = lax.ppermute(amplitudes, "core", SWAP)

    right_moved = lax.ppermute(aux_right.T, ALL, chips(0, to_row))
    right_rows = spread(right_moved, AUX_COL, 16).reshape(1024, cols)

    partial = lax.dot_general(
        left_kept, amplitudes, (((1,), (1,)), ((), ())), preferred_element_type=jnp.float32
    ) + lax.dot_general(
        left_taken, other_amplitudes, (((1,), (1,)), ((), ())), preferred_element_type=jnp.float32
    )
    sent = (partial * X_SCALE).astype(jnp.float16).reshape(4, 128, rows)
    sent, right_rows = lax.optimization_barrier((sent, right_rows))
    right_rows_other = lax.ppermute(right_rows, "core", SWAP)
    right_rows = jnp.concatenate(
        [
            jnp.where(first, right_rows, right_rows_other),
            jnp.where(first, right_rows_other, right_rows),
        ],
        axis=1,
    )
    summed = jnp.sum(lax.all_to_all(sent, "x", 0, 0).astype(jnp.float32), axis=0)
    sent = (summed * (Z_SCALE / X_SCALE)).astype(jnp.float16).reshape(4, 32, rows)
    sent, right_rows = lax.optimization_barrier((sent, right_rows))
    summed = jnp.sum(lax.all_to_all(sent, "zl", 0, 0).astype(jnp.float32), axis=0)
    fitted = (summed * (1.0 / Z_SCALE)).astype(jnp.bfloat16)

    fitted_half = spread(fitted, AUX_COL, 16).reshape(512, rows)
    light = (fitted.astype(jnp.float32) * FIT_SCALE).astype(jnp.float16)
    light_kept = lax.dynamic_slice_in_dim(light, core * cols, cols, 1)
    light_given = lax.dynamic_slice_in_dim(light, (1 - core) * cols, cols, 1)
    copies = []
    for far in (0, 1):
        same = lax.ppermute(light_kept, ALL, chips(0, to_column, far))
        cross = lax.ppermute(light_given, ALL, chips(1, to_column, far))
        copies += [jnp.where(first, same, cross), jnp.where(first, cross, same)]
    mirror_chunk = jnp.stack(copies).reshape(2, 64, cols)
    mirror = lax.all_gather(mirror_chunk, "y", axis=0, tiled=True).reshape(1024, cols)
    mirror, fitted_half = lax.optimization_barrier((mirror, fitted_half))
    fitted_other = lax.ppermute(fitted_half, "core", SWAP)
    mirror = restore(mirror, FIT_SCALE)

    mixed = contract(fitted_half, right_kept) + contract(fitted_other, right_other)
    mirrored = contract(right_rows, mirror)
    row_gap = pair_gap(
        occupied_map, virtual_map, occupied_energy, virtual_energy, row_block * rows, rows
    )
    col_gap = pair_gap(
        occupied_map, virtual_map, occupied_energy, virtual_energy, col_block * cols, cols
    )
    return (mixed + mirrored) / (row_gap[:, None] + col_gap[None, :])


def solution(mesh):
    fine = Mesh(mesh.devices.reshape(SIZES), ALL)
    by_block = P(ROW, COL + ("core",))
    by_aux = P(COL + ("core",), ROW)
    return jax.shard_map(
        per_device,
        mesh=fine,
        in_specs=(by_block, by_aux, by_aux, P(), P(), P(), P()),
        out_specs=by_block,
        check_vma=False,
    )
```

```python
import itertools

import jax
import jax.numpy as jnp
from jax import lax
from jax.sharding import Mesh
from jax.sharding import PartitionSpec as P

ROW = ("zh", "y")
COL = ("zl", "x")
AUX_COL = ("x", "zl")
ALL = ("zh", "y", "zl", "x", "core")
SIZES = (2, 8, 4, 4, 2)
SWAP = [(0, 1), (1, 0)]
LEFT_SCALE = 2.0**20
RIGHT_SCALE = 2.0**18
FIT_SCALE = 8.0
SUM_SCALE = 128.0


def device_of(zh, y, zl, x, core):
    return (((zh * 8 + y) * 4 + zl) * 4 + x) * 2 + core


def chips(move, far=0):
    pairs = []
    for zh, y, zl, x, core in itertools.product(*(range(n) for n in SIZES)):
        to_zh, *rest = move(zh, y, zl, x)
        pairs.append((device_of(zh, y, zl, x, core), device_of(to_zh ^ far, *rest, core)))
    return pairs


def to_column(zh, y, zl, x):
    slot, block = x * 4 + zl, zh * 8 + y
    return slot & 1, slot >> 1, block // 4, block % 4


def to_row(zh, y, zl, x):
    slot, block = y * 2 + zh, zl * 4 + x
    return block // 8, block % 8, slot % 4, slot // 4


def pack(values, scale):
    return (values.astype(jnp.float32) * scale).astype(jnp.float16)


def restore(values, scale):
    return (values.astype(jnp.float32) * (1.0 / scale)).astype(jnp.bfloat16)


def lookup(positions, energy_table):
    matches = positions[:, None] == jnp.arange(energy_table.shape[0], dtype=jnp.int32)[None, :]
    return jnp.sum(jnp.where(matches, energy_table[None, :], 0.0), axis=1)


def pair_gap(occupied_map, virtual_map, occupied_energy, virtual_energy, offset, length):
    occupied_part = lax.dynamic_slice_in_dim(occupied_map, offset, length, 0)
    virtual_part = lax.dynamic_slice_in_dim(virtual_map, offset, length, 0)
    return lookup(virtual_part, virtual_energy) - lookup(occupied_part, occupied_energy)


def contract(left, right):
    return lax.dot_general(
        left, right, (((0,), (0,)), ((), ())), preferred_element_type=jnp.float32
    )


def per_device(
    amplitudes, aux_left, aux_right, occupied_map, virtual_map, occupied_energy, virtual_energy
):
    rows, cols = amplitudes.shape
    core = lax.axis_index("core")
    first = core == 0
    row_block = lax.axis_index(ROW)
    col_block = lax.axis_index(COL + ("core",))

    left = pack(aux_left.T, LEFT_SCALE)
    right = pack(aux_right.T, RIGHT_SCALE)
    near = lax.all_gather(jnp.concatenate([left, right], axis=0), ("zh", "core"), axis=0)
    near = near.reshape(2, 2, 2 * left.shape[0], cols)
    mine = lax.dynamic_index_in_dim(near, core, 1, keepdims=False)
    theirs = lax.dynamic_index_in_dim(near, 1 - core, 1, keepdims=False)
    chunk = jnp.concatenate(
        [
            lax.dynamic_slice_in_dim(mine, core * 32, 32, 1),
            lax.dynamic_slice_in_dim(theirs, core * 32, 32, 1),
            mine[:, 64:],
        ],
        axis=1,
    )
    factors = lax.all_gather(chunk, "y", axis=0, tiled=True)
    left_kept = restore(factors[:, :32], LEFT_SCALE).reshape(512, cols)
    left_taken = restore(factors[:, 32:64], LEFT_SCALE).reshape(512, cols)
    right_cols = restore(factors[:, 64:], RIGHT_SCALE).reshape(1024, cols)
    other_amplitudes = lax.ppermute(amplitudes, "core", SWAP)

    partial = lax.dot_general(
        left_kept, amplitudes, (((1,), (1,)), ((), ())), preferred_element_type=jnp.float32
    ) + lax.dot_general(
        left_taken, other_amplitudes, (((1,), (1,)), ((), ())), preferred_element_type=jnp.float32
    )
    sent = (partial * SUM_SCALE).astype(jnp.float16).reshape(16, 32, rows)
    right_moved = lax.ppermute(right, ALL, chips(to_row))
    arrived = lax.all_to_all(sent, AUX_COL, 0, 0)
    arrived, right_moved = lax.optimization_barrier((arrived, right_moved))
    summed = jnp.sum(arrived.astype(jnp.float32), axis=0) * (1.0 / SUM_SCALE)
    fitted = pack(summed.astype(jnp.bfloat16), FIT_SCALE)

    kept = lax.dynamic_slice_in_dim(fitted, core * cols, cols, 1)
    given = lax.dynamic_slice_in_dim(fitted, (1 - core) * cols, cols, 1)
    taken = lax.ppermute(given, "core", SWAP)
    fitted = jnp.concatenate(
        [jnp.where(first, kept, taken), jnp.where(first, taken, kept)], axis=0
    )
    same = lax.ppermute(fitted, ALL, chips(to_column))
    cross = lax.ppermute(fitted, ALL, chips(to_column, 1))
    both = lax.all_gather(jnp.stack([right_moved, fitted]), "zl", axis=0)
    both, same, cross = lax.optimization_barrier((both, same, cross))
    low = lax.axis_index("zh") == 0
    mirror_chunk = jnp.stack([jnp.where(low, same, cross), jnp.where(low, cross, same)])
    mirror = lax.all_gather(mirror_chunk, "y", axis=0, tiled=True)
    mirror = restore(mirror, FIT_SCALE).reshape(1024, cols)
    both = lax.all_gather(both, ("x", "core"), axis=0).reshape(4, 2, 4, 2, 64, cols)

    halves = []
    for half in range(2):
        right_rows = restore(both[:, half, :, 0], RIGHT_SCALE).reshape(1024, cols)
        fitted_rows = restore(both[:, half, :, 1], FIT_SCALE).reshape(1024, cols)
        halves.append(contract(fitted_rows, right_cols) + contract(right_rows, mirror))
    total = jnp.concatenate(halves, axis=0)
    row_gap = pair_gap(
        occupied_map, virtual_map, occupied_energy, virtual_energy, row_block * rows, rows
    )
    col_gap = pair_gap(
        occupied_map, virtual_map, occupied_energy, virtual_energy, col_block * cols, cols
    )
    return total / (row_gap[:, None] + col_gap[None, :])


def solution(mesh):
    fine = Mesh(mesh.devices.reshape(SIZES), ALL)
    by_block = P(ROW, COL + ("core",))
    by_aux = P(COL + ("core",), ROW)
    return jax.shard_map(
        per_device,
        mesh=fine,
        in_specs=(by_block, by_aux, by_aux, P(), P(), P(), P()),
        out_specs=by_block,
        check_vma=False,
    )
```

```python
import itertools

import jax
import jax.numpy as jnp
from jax import lax
from jax.sharding import Mesh
from jax.sharding import PartitionSpec as P

ROW = ("zh", "y")
COL = ("zl", "x")
AUX_COL = ("x", "zl")
ALL = ("zh", "y", "zl", "x", "core")
SIZES = (2, 8, 4, 4, 2)
SWAP = [(0, 1), (1, 0)]
LEFT_SCALE = 2.0**20
RIGHT_SCALE = 2.0**18
FIT_SCALE = 8.0
SUM_SCALE = 128.0


def device_of(zh, y, zl, x, core):
    return (((zh * 8 + y) * 4 + zl) * 4 + x) * 2 + core


def chips(move, far=0):
    pairs = []
    for zh, y, zl, x, core in itertools.product(*(range(n) for n in SIZES)):
        to_zh, *rest = move(zh, y, zl, x)
        pairs.append((device_of(zh, y, zl, x, core), device_of(to_zh ^ far, *rest, core)))
    return pairs


def to_column(zh, y, zl, x):
    slot, block = x * 4 + zl, zh * 8 + y
    return slot & 1, slot >> 1, block // 4, block % 4


def to_row(zh, y, zl, x):
    slot, block = y * 2 + zh, zl * 4 + x
    return block // 8, block % 8, slot % 4, slot // 4


def pack(values, scale):
    return (values.astype(jnp.float32) * scale).astype(jnp.float16)


def restore(values, scale):
    return (values.astype(jnp.float32) * (1.0 / scale)).astype(jnp.bfloat16)


def lookup(positions, energy_table):
    matches = positions[:, None] == jnp.arange(energy_table.shape[0], dtype=jnp.int32)[None, :]
    return jnp.sum(jnp.where(matches, energy_table[None, :], 0.0), axis=1)


def pair_gap(occupied_map, virtual_map, occupied_energy, virtual_energy, offset, length):
    occupied_part = lax.dynamic_slice_in_dim(occupied_map, offset, length, 0)
    virtual_part = lax.dynamic_slice_in_dim(virtual_map, offset, length, 0)
    return lookup(virtual_part, virtual_energy) - lookup(occupied_part, occupied_energy)


def contract(left, right):
    return lax.dot_general(
        left, right, (((0,), (0,)), ((), ())), preferred_element_type=jnp.float32
    )


def per_device(
    amplitudes, aux_left, aux_right, occupied_map, virtual_map, occupied_energy, virtual_energy
):
    rows, cols = amplitudes.shape
    core = lax.axis_index("core")
    row_block = lax.axis_index(ROW)
    col_block = lax.axis_index(COL + ("core",))

    left = pack(aux_left.T, LEFT_SCALE)
    right = pack(aux_right.T, RIGHT_SCALE)
    near = lax.all_gather(jnp.concatenate([left, right], axis=0), ("zh", "core"), axis=0)
    near = near.reshape(2, 2, 2 * left.shape[0], cols)
    mine = lax.dynamic_index_in_dim(near, core, 1, keepdims=False)
    theirs = lax.dynamic_index_in_dim(near, 1 - core, 1, keepdims=False)
    chunk = jnp.concatenate(
        [
            lax.dynamic_slice_in_dim(mine, core * 32, 32, 1),
            lax.dynamic_slice_in_dim(theirs, core * 32, 32, 1),
            mine[:, 64:],
        ],
        axis=1,
    )
    factors = lax.all_gather(chunk, "y", axis=0, tiled=True)
    left_kept = restore(factors[:, :32], LEFT_SCALE).reshape(512, cols)
    left_taken = restore(factors[:, 32:64], LEFT_SCALE).reshape(512, cols)
    right_cols = restore(factors[:, 64:], RIGHT_SCALE).reshape(4, 4, 2, 32, cols)
    right_cols = right_cols.transpose(0, 2, 1, 3, 4).reshape(1024, cols)
    other_amplitudes = lax.ppermute(amplitudes, "core", SWAP)

    partial = lax.dot_general(
        left_kept, amplitudes, (((1,), (1,)), ((), ())), preferred_element_type=jnp.float32
    ) + lax.dot_general(
        left_taken, other_amplitudes, (((1,), (1,)), ((), ())), preferred_element_type=jnp.float32
    )
    sent = (partial * SUM_SCALE).astype(jnp.float16).reshape(16, 32, rows)
    right_moved = lax.ppermute(right, ALL, chips(to_row))
    arrived = lax.all_to_all(sent, AUX_COL, 0, 0)
    arrived, right_moved = lax.optimization_barrier((arrived, right_moved))
    summed = jnp.sum(arrived.astype(jnp.float32), axis=0) * (1.0 / SUM_SCALE)
    rounded = lax.reduce_precision(summed, exponent_bits=8, mantissa_bits=7)
    fitted = rounded.astype(jnp.bfloat16)
    light = (rounded * FIT_SCALE).astype(jnp.float16)
    light = jnp.concatenate([light[:, :cols], light[:, cols:]], axis=0)

    same = lax.ppermute(fitted, ALL, chips(to_column))
    cross = lax.ppermute(fitted, ALL, chips(to_column, 1))
    both = lax.all_gather(jnp.concatenate([right_moved, light], axis=0), "zl", axis=0)
    both, same, cross = lax.optimization_barrier((both, same, cross))
    both = both.reshape(2, 2, 4, 32, cols)
    right_part = both[:, :, :2].transpose(0, 2, 1, 3, 4).reshape(256, cols)
    fitted_part = both[:, :, 2:].transpose(2, 0, 1, 3, 4).reshape(256, cols)
    both = jnp.concatenate([right_part, fitted_part], axis=0)
    low = lax.axis_index("zh") == 0
    below, above = jnp.where(low, same, cross), jnp.where(low, cross, same)
    mirror_chunk = jnp.stack(
        [below[:, :cols], above[:, :cols], below[:, cols:], above[:, cols:]]
    )
    mirror = jnp.broadcast_to(mirror_chunk[None], (8,) + mirror_chunk.shape)
    mirror = lax.all_to_all(mirror.reshape(16, 2, 32, cols), ("y", "core"), 0, 0)
    both = lax.all_gather(both, ("x", "core"), axis=0).reshape(4, 2, 512, cols)
    mirror = mirror.reshape(1024, cols)

    halves = []
    for half in range(2):
        right_rows = restore(both[:, half, :256], RIGHT_SCALE).reshape(1024, cols)
        start = 256 + half * 128
        fitted_rows = restore(both[:, :, start : start + 128], FIT_SCALE).reshape(1024, cols)
        halves.append(contract(fitted_rows, right_cols) + contract(right_rows, mirror))
    total = jnp.concatenate(halves, axis=0)
    row_gap = pair_gap(
        occupied_map, virtual_map, occupied_energy, virtual_energy, row_block * rows, rows
    )
    col_gap = pair_gap(
        occupied_map, virtual_map, occupied_energy, virtual_energy, col_block * cols, cols
    )
    return total / (row_gap[:, None] + col_gap[None, :])


def solution(mesh):
    fine = Mesh(mesh.devices.reshape(SIZES), ALL)
    by_block = P(ROW, COL + ("core",))
    by_aux = P(COL + ("core",), ROW)
    return jax.shard_map(
        per_device,
        mesh=fine,
        in_specs=(by_block, by_aux, by_aux, P(), P(), P(), P()),
        out_specs=by_block,
        check_vma=False,
    )
```

```python
import itertools

import jax
import jax.numpy as jnp
from jax import lax
from jax.sharding import Mesh
from jax.sharding import PartitionSpec as P

ROW = ("zh", "y")
COL = ("zl", "x")
AUX_COL = ("x", "zl")
ALL = ("zh", "y", "zl", "x", "core")
SIZES = (2, 8, 4, 4, 2)
SWAP = [(0, 1), (1, 0)]
LEFT_SCALE = 2.0**20
RIGHT_SCALE = 2.0**18
FIT_SCALE = 8.0
SUM_SCALE = 128.0


def device_of(zh, y, zl, x, core):
    return (((zh * 8 + y) * 4 + zl) * 4 + x) * 2 + core


def chips(move, far=0):
    pairs = []
    for zh, y, zl, x, core in itertools.product(*(range(n) for n in SIZES)):
        to_zh, *rest = move(zh, y, zl, x)
        pairs.append((device_of(zh, y, zl, x, core), device_of(to_zh ^ far, *rest, core)))
    return pairs


def to_column(zh, y, zl, x):
    slot, block = x * 4 + zl, zh * 8 + y
    return slot & 1, slot >> 1, block // 4, block % 4


def to_row(zh, y, zl, x):
    slot, block = y * 2 + zh, zl * 4 + x
    return block // 8, block % 8, slot % 4, slot // 4


def pack(values, scale):
    return (values.astype(jnp.float32) * scale).astype(jnp.float16)


def restore(values, scale):
    return (values.astype(jnp.float32) * (1.0 / scale)).astype(jnp.bfloat16)


def lookup(positions, energy_table):
    matches = positions[:, None] == jnp.arange(energy_table.shape[0], dtype=jnp.int32)[None, :]
    return jnp.sum(jnp.where(matches, energy_table[None, :], 0.0), axis=1)


def pair_gap(occupied_map, virtual_map, occupied_energy, virtual_energy, offset, length):
    occupied_part = lax.dynamic_slice_in_dim(occupied_map, offset, length, 0)
    virtual_part = lax.dynamic_slice_in_dim(virtual_map, offset, length, 0)
    return lookup(virtual_part, virtual_energy) - lookup(occupied_part, occupied_energy)


def contract(left, right):
    return lax.dot_general(
        left, right, (((0,), (0,)), ((), ())), preferred_element_type=jnp.float32
    )


def per_device(
    amplitudes, aux_left, aux_right, occupied_map, virtual_map, occupied_energy, virtual_energy
):
    rows, cols = amplitudes.shape
    core = lax.axis_index("core")
    row_block = lax.axis_index(ROW)
    col_block = lax.axis_index(COL + ("core",))

    pair = jnp.concatenate([aux_left.T, aux_right.T], axis=0)
    near = lax.all_gather(pair, ("zh", "core"), axis=0).reshape(2, 2, 128, cols)
    mine = lax.dynamic_index_in_dim(near, core, 1, keepdims=False)
    theirs = lax.dynamic_index_in_dim(near, 1 - core, 1, keepdims=False)
    left_near = jnp.concatenate(
        [
            lax.dynamic_slice_in_dim(mine, core * 32, 32, 1),
            lax.dynamic_slice_in_dim(theirs, core * 32, 32, 1),
        ],
        axis=1,
    )
    chunk = jnp.concatenate(
        [pack(left_near, LEFT_SCALE), pack(mine[:, 64:], RIGHT_SCALE)], axis=1
    )
    factors = lax.all_gather(chunk, "y", axis=0, tiled=True)
    left_kept = restore(factors[:, :32], LEFT_SCALE).reshape(512, cols)
    left_taken = restore(factors[:, 32:64], LEFT_SCALE).reshape(512, cols)
    right_cols = restore(factors[:, 64:], RIGHT_SCALE).reshape(4, 4, 2, 32, cols)
    right_cols = right_cols.transpose(0, 2, 1, 3, 4).reshape(1024, cols)
    other_amplitudes = lax.ppermute(amplitudes, "core", SWAP)

    partial = lax.dot_general(
        left_kept, amplitudes, (((1,), (1,)), ((), ())), preferred_element_type=jnp.float32
    ) + lax.dot_general(
        left_taken, other_amplitudes, (((1,), (1,)), ((), ())), preferred_element_type=jnp.float32
    )
    sent = (partial * SUM_SCALE).astype(jnp.float16).reshape(16, 32, rows)
    right_moved = lax.ppermute(pack(aux_right.T, RIGHT_SCALE), ALL, chips(to_row))
    arrived = lax.all_to_all(sent, AUX_COL, 0, 0)
    arrived, right_moved = lax.optimization_barrier((arrived, right_moved))
    summed = jnp.sum(arrived.astype(jnp.float32), axis=0) * (1.0 / SUM_SCALE)
    rounded = lax.reduce_precision(summed, exponent_bits=8, mantissa_bits=7)
    fitted = rounded.astype(jnp.bfloat16)
    light = (rounded * FIT_SCALE).astype(jnp.float16)
    light = jnp.concatenate([light[:, :cols], light[:, cols:]], axis=0)

    same = lax.ppermute(fitted, ALL, chips(to_column))
    cross = lax.ppermute(fitted, ALL, chips(to_column, 1))
    low = lax.axis_index("zh") == 0
    below, above = jnp.where(low, same, cross), jnp.where(low, cross, same)
    mirror_chunk = jnp.stack(
        [below[:, :cols], above[:, :cols], below[:, cols:], above[:, cols:]]
    )
    mirror = jnp.broadcast_to(mirror_chunk[None], (8,) + mirror_chunk.shape)
    mirror = lax.all_to_all(mirror.reshape(16, 2, 32, cols), ("y", "core"), 0, 0)
    both = lax.all_gather(jnp.concatenate([right_moved, light], axis=0), "zl", axis=0)
    both = both.reshape(2, 2, 4, 32, cols)
    right_part = both[:, :, :2].transpose(0, 2, 1, 3, 4).reshape(256, cols)
    fitted_part = both[:, :, 2:].transpose(2, 0, 1, 3, 4).reshape(256, cols)
    both = jnp.concatenate([right_part, fitted_part], axis=0)
    both = lax.all_gather(both, ("x", "core"), axis=0).reshape(4, 2, 512, cols)
    mirror = mirror.reshape(1024, cols)

    halves = []
    for half in range(2):
        right_rows = restore(both[:, half, :256], RIGHT_SCALE).reshape(1024, cols)
        start = 256 + half * 128
        fitted_rows = restore(both[:, :, start : start + 128], FIT_SCALE).reshape(1024, cols)
        halves.append(contract(fitted_rows, right_cols) + contract(right_rows, mirror))
    total = jnp.concatenate(halves, axis=0)
    row_gap = pair_gap(
        occupied_map, virtual_map, occupied_energy, virtual_energy, row_block * rows, rows
    )
    col_gap = pair_gap(
        occupied_map, virtual_map, occupied_energy, virtual_energy, col_block * cols, cols
    )
    return total / (row_gap[:, None] + col_gap[None, :])


def solution(mesh):
    fine = Mesh(mesh.devices.reshape(SIZES), ALL)
    by_block = P(ROW, COL + ("core",))
    by_aux = P(COL + ("core",), ROW)
    return jax.shard_map(
        per_device,
        mesh=fine,
        in_specs=(by_block, by_aux, by_aux, P(), P(), P(), P()),
        out_specs=by_block,
        check_vma=False,
    )
```

```python
import itertools

import jax
import jax.numpy as jnp
from jax import lax
from jax.sharding import Mesh
from jax.sharding import PartitionSpec as P

ROW = ("zh", "y")
COL = ("zl", "x")
AUX_COL = ("x", "zl")
ALL = ("zh", "y", "zl", "x", "core")
SIZES = (2, 8, 4, 4, 2)
SWAP = [(0, 1), (1, 0)]
LEFT_SCALE = 2.0**20
RIGHT_SCALE = 2.0**18
FIT_SCALE = 8.0
SUM_SCALE = 128.0


def device_of(zh, y, zl, x, core):
    return (((zh * 8 + y) * 4 + zl) * 4 + x) * 2 + core


def moves(step):
    pairs = []
    for place in itertools.product(*(range(n) for n in SIZES)):
        pairs.append((device_of(*place), device_of(*step(*place))))
    return pairs


def to_column(zh, y, zl, x, core):
    slot, block = x * 4 + zl, zh * 8 + y
    return core, slot >> 1, block // 4, block % 4, slot & 1


def to_row(zh, y, zl, x, core):
    slot, block = y * 2 + zh, zl * 4 + x
    return block // 8, block % 8, slot % 4, slot // 4, core


def pack(values, scale):
    return (values.astype(jnp.float32) * scale).astype(jnp.float16)


def restore(values, scale):
    return (values.astype(jnp.float32) * (1.0 / scale)).astype(jnp.bfloat16)


def lookup(positions, energy_table):
    matches = positions[:, None] == jnp.arange(energy_table.shape[0], dtype=jnp.int32)[None, :]
    return jnp.sum(jnp.where(matches, energy_table[None, :], 0.0), axis=1)


def pair_gap(occupied_map, virtual_map, occupied_energy, virtual_energy, offset, length):
    occupied_part = lax.dynamic_slice_in_dim(occupied_map, offset, length, 0)
    virtual_part = lax.dynamic_slice_in_dim(virtual_map, offset, length, 0)
    return lookup(virtual_part, virtual_energy) - lookup(occupied_part, occupied_energy)


def contract(left, right):
    return lax.dot_general(
        left, right, (((0,), (0,)), ((), ())), preferred_element_type=jnp.float32
    )


def per_device(
    amplitudes, aux_left, aux_right, occupied_map, virtual_map, occupied_energy, virtual_energy
):
    rows, cols = amplitudes.shape
    core = lax.axis_index("core")
    first = core == 0
    row_block = lax.axis_index(ROW)
    col_block = lax.axis_index(COL + ("core",))

    pair = jnp.concatenate([aux_left.T, aux_right.T], axis=0)
    near = lax.all_gather(pair, ("zh", "core"), axis=0).reshape(2, 2, 128, cols)
    mine = lax.dynamic_index_in_dim(near, core, 1, keepdims=False)
    theirs = lax.dynamic_index_in_dim(near, 1 - core, 1, keepdims=False)
    left_near = jnp.concatenate(
        [
            lax.dynamic_slice_in_dim(mine, core * 32, 32, 1),
            lax.dynamic_slice_in_dim(theirs, core * 32, 32, 1),
        ],
        axis=1,
    )
    chunk = jnp.concatenate(
        [pack(left_near, LEFT_SCALE), pack(mine[:, 64:], RIGHT_SCALE)], axis=1
    )
    factors = lax.all_gather(chunk, "y", axis=0, tiled=True)
    left_kept = restore(factors[:, :32], LEFT_SCALE).reshape(512, cols)
    left_taken = restore(factors[:, 32:64], LEFT_SCALE).reshape(512, cols)
    right_cols = restore(factors[:, 64:], RIGHT_SCALE).reshape(1024, cols)
    other_amplitudes = lax.ppermute(amplitudes, "core", SWAP)

    partial = lax.dot_general(
        left_kept, amplitudes, (((1,), (1,)), ((), ())), preferred_element_type=jnp.float32
    ) + lax.dot_general(
        left_taken, other_amplitudes, (((1,), (1,)), ((), ())), preferred_element_type=jnp.float32
    )
    sent = (partial * SUM_SCALE).astype(jnp.float16).reshape(16, 32, rows)
    right_moved = lax.ppermute(pack(aux_right.T, RIGHT_SCALE), ALL, moves(to_row))
    arrived = lax.all_to_all(sent, AUX_COL, 0, 0)
    arrived, right_moved = lax.optimization_barrier((arrived, right_moved))
    summed = jnp.sum(arrived.astype(jnp.float32), axis=0) * (1.0 / SUM_SCALE)
    rounded = lax.reduce_precision(summed, exponent_bits=8, mantissa_bits=7)
    fitted = rounded.astype(jnp.bfloat16)
    swapped = lax.ppermute(fitted, "core", SWAP)
    fitted = jnp.concatenate(
        [jnp.where(first, fitted, swapped), jnp.where(first, swapped, fitted)], axis=0
    )
    moved = lax.ppermute(fitted, ALL, moves(to_column))
    light = pack(lax.dynamic_slice_in_dim(fitted, core * cols, cols, 1), FIT_SCALE)
    both = lax.all_gather(jnp.stack([right_moved, light]), "zl", axis=0)
    both, moved = lax.optimization_barrier((both, moved))
    mirror = jnp.stack([moved[:, :cols], moved[:, cols:]])
    mirror = jnp.broadcast_to(mirror[None], (8, 2, 64, cols)).reshape(16, 64, cols)
    mirror = lax.all_to_all(mirror, ("y", "core"), 0, 0).reshape(1024, cols)
    both = lax.all_gather(both, ("x", "core"), axis=0).reshape(4, 2, 4, 2, 64, cols)

    halves = []
    for half in range(2):
        right_rows = restore(both[:, half, :, 0], RIGHT_SCALE).reshape(1024, cols)
        fitted_rows = restore(both[:, half, :, 1], FIT_SCALE).reshape(1024, cols)
        halves.append(contract(fitted_rows, right_cols) + contract(right_rows, mirror))
    total = jnp.concatenate(halves, axis=0)
    row_gap = pair_gap(
        occupied_map, virtual_map, occupied_energy, virtual_energy, row_block * rows, rows
    )
    col_gap = pair_gap(
        occupied_map, virtual_map, occupied_energy, virtual_energy, col_block * cols, cols
    )
    return total / (row_gap[:, None] + col_gap[None, :])


def solution(mesh):
    fine = Mesh(mesh.devices.reshape(SIZES), ALL)
    by_block = P(ROW, COL + ("core",))
    by_aux = P(COL + ("core",), ROW)
    return jax.shard_map(
        per_device,
        mesh=fine,
        in_specs=(by_block, by_aux, by_aux, P(), P(), P(), P()),
        out_specs=by_block,
        check_vma=False,
    )
```

```python
import itertools

import jax
import jax.numpy as jnp
from jax import lax
from jax.sharding import Mesh
from jax.sharding import PartitionSpec as P

ROW = ("zh", "y")
COL = ("zl", "x")
ALL = ("zh", "y", "zl", "x", "core")
SIZES = (2, 8, 4, 4, 2)
SWAP = [(0, 1), (1, 0)]
LEFT_SCALE = 2.0**20
RIGHT_SCALE = 2.0**18
FIT_SCALE = 8.0
SUM_SCALE = 128.0
LINE_SCALE = 32.0


def device_of(zh, y, zl, x, core):
    return (((zh * 8 + y) * 4 + zl) * 4 + x) * 2 + core


def chips(move, far=0):
    pairs = []
    for zh, y, zl, x, core in itertools.product(*(range(n) for n in SIZES)):
        to_zh, *rest = move(zh, y, zl, x)
        pairs.append((device_of(zh, y, zl, x, core), device_of(to_zh ^ far, *rest, core)))
    return pairs


def to_column(zh, y, zl, x):
    block = zh * 8 + y
    return x >> 1, zl * 2 + (x & 1), block // 4, block % 4


def to_row(zh, y, zl, x):
    slot, block = y * 2 + zh, zl * 4 + x
    return block // 8, block % 8, slot % 4, slot // 4


def pack(values, scale):
    return (values.astype(jnp.float32) * scale).astype(jnp.float16)


def restore(values, scale):
    return (values.astype(jnp.float32) * (1.0 / scale)).astype(jnp.bfloat16)


def lookup(positions, energy_table):
    matches = positions[:, None] == jnp.arange(energy_table.shape[0], dtype=jnp.int32)[None, :]
    return jnp.sum(jnp.where(matches, energy_table[None, :], 0.0), axis=1)


def pair_gap(occupied_map, virtual_map, occupied_energy, virtual_energy, offset, length):
    occupied_part = lax.dynamic_slice_in_dim(occupied_map, offset, length, 0)
    virtual_part = lax.dynamic_slice_in_dim(virtual_map, offset, length, 0)
    return lookup(virtual_part, virtual_energy) - lookup(occupied_part, occupied_energy)


def contract(left, right):
    return lax.dot_general(
        left, right, (((0,), (0,)), ((), ())), preferred_element_type=jnp.float32
    )


def per_device(
    amplitudes, aux_left, aux_right, occupied_map, virtual_map, occupied_energy, virtual_energy
):
    rows, cols = amplitudes.shape
    core = lax.axis_index("core")
    row_block = lax.axis_index(ROW)
    col_block = lax.axis_index(COL + ("core",))

    pair = jnp.concatenate([aux_left.T, aux_right.T], axis=0)
    near = lax.all_gather(pair, ("zh", "core"), axis=0).reshape(2, 2, 128, cols)
    mine = lax.dynamic_index_in_dim(near, core, 1, keepdims=False)
    theirs = lax.dynamic_index_in_dim(near, 1 - core, 1, keepdims=False)
    left_near = jnp.concatenate(
        [
            lax.dynamic_slice_in_dim(mine, core * 32, 32, 1),
            lax.dynamic_slice_in_dim(theirs, core * 32, 32, 1),
        ],
        axis=1,
    )
    chunk = jnp.concatenate(
        [pack(left_near, LEFT_SCALE), pack(mine[:, 64:], RIGHT_SCALE)], axis=1
    )
    factors = lax.all_gather(chunk, "y", axis=0, tiled=True)
    factors = factors.reshape(2, 2, 2, 2, 128, cols)
    by_slot = factors.transpose(3, 2, 0, 1, 4, 5)
    left_kept = restore(by_slot[..., :32, :], LEFT_SCALE).reshape(512, cols)
    left_taken = restore(by_slot[..., 32:64, :], LEFT_SCALE).reshape(512, cols)
    right_cols = by_slot[..., 64:, :].reshape(4, 4, 2, 32, cols).transpose(0, 2, 1, 3, 4)
    right_cols = restore(right_cols, RIGHT_SCALE).reshape(1024, cols)
    other_amplitudes = lax.ppermute(amplitudes, "core", SWAP)

    partial = lax.dot_general(
        left_kept, amplitudes, (((1,), (1,)), ((), ())), preferred_element_type=jnp.float32
    ) + lax.dot_general(
        left_taken, other_amplitudes, (((1,), (1,)), ((), ())), preferred_element_type=jnp.float32
    )
    sent = (partial * SUM_SCALE).astype(jnp.float16).reshape(4, 128, rows)
    right_moved = lax.ppermute(pack(aux_right.T, RIGHT_SCALE), ALL, chips(to_row))
    arrived = lax.all_to_all(sent, "x", 0, 0)
    summed = jnp.sum(arrived.astype(jnp.float32), axis=0) * (LINE_SCALE / SUM_SCALE)
    sent = summed.astype(jnp.float16).reshape(4, 32, rows)
    arrived = lax.all_to_all(sent, "zl", 0, 0)
    arrived, right_moved = lax.optimization_barrier((arrived, right_moved))
    summed = jnp.sum(arrived.astype(jnp.float32), axis=0) * (1.0 / LINE_SCALE)
    rounded = lax.reduce_precision(summed, exponent_bits=8, mantissa_bits=7)
    fitted = rounded.astype(jnp.bfloat16)
    light = (rounded * FIT_SCALE).astype(jnp.float16)
    light = jnp.concatenate([light[:, :cols], light[:, cols:]], axis=0)

    same = lax.ppermute(fitted, ALL, chips(to_column))
    cross = lax.ppermute(fitted, ALL, chips(to_column, 1))
    both = lax.all_gather(jnp.concatenate([right_moved, light], axis=0), "zl", axis=0)
    both, same, cross = lax.optimization_barrier((both, same, cross))
    both = both.reshape(2, 2, 4, 32, cols)
    right_part = both[:, :, :2].transpose(0, 2, 1, 3, 4).reshape(256, cols)
    fitted_part = both[:, :, 2:].transpose(2, 0, 1, 3, 4).reshape(256, cols)
    both = jnp.concatenate([right_part, fitted_part], axis=0)
    low = lax.axis_index("zh") == 0
    below, above = jnp.where(low, same, cross), jnp.where(low, cross, same)
    mirror_chunk = jnp.stack(
        [below[:, :cols], above[:, :cols], below[:, cols:], above[:, cols:]]
    )
    mirror = jnp.broadcast_to(mirror_chunk[None], (8,) + mirror_chunk.shape)
    mirror = lax.all_to_all(mirror.reshape(16, 2, 32, cols), ("y", "core"), 0, 0)
    both = lax.all_gather(both, ("x", "core"), axis=0).reshape(4, 2, 512, cols)
    mirror = mirror.reshape(1024, cols)

    halves = []
    for half in range(2):
        right_rows = restore(both[:, half, :256], RIGHT_SCALE).reshape(1024, cols)
        start = 256 + half * 128
        fitted_rows = restore(both[:, :, start : start + 128], FIT_SCALE).reshape(1024, cols)
        halves.append(contract(fitted_rows, right_cols) + contract(right_rows, mirror))
    total = jnp.concatenate(halves, axis=0)
    row_gap = pair_gap(
        occupied_map, virtual_map, occupied_energy, virtual_energy, row_block * rows, rows
    )
    col_gap = pair_gap(
        occupied_map, virtual_map, occupied_energy, virtual_energy, col_block * cols, cols
    )
    return total / (row_gap[:, None] + col_gap[None, :])


def solution(mesh):
    fine = Mesh(mesh.devices.reshape(SIZES), ALL)
    by_block = P(ROW, COL + ("core",))
    by_aux = P(COL + ("core",), ROW)
    return jax.shard_map(
        per_device,
        mesh=fine,
        in_specs=(by_block, by_aux, by_aux, P(), P(), P(), P()),
        out_specs=by_block,
        check_vma=False,
    )
```

```python
import itertools

import jax
import jax.numpy as jnp
from jax import lax
from jax.sharding import Mesh
from jax.sharding import PartitionSpec as P

ROW = ("zh", "y")
COL = ("zl", "x")
ALL = ("zh", "y", "zl", "x", "core")
SIZES = (2, 8, 4, 4, 2)
SWAP = [(0, 1), (1, 0)]
LEFT_SCALE = 2.0**20
RIGHT_SCALE = 2.0**18
FIT_SCALE = 8.0
SUM_SCALE = 128.0
LINE_SCALE = 32.0


def device_of(zh, y, zl, x, core):
    return (((zh * 8 + y) * 4 + zl) * 4 + x) * 2 + core


def chips(move, far=0):
    pairs = []
    for zh, y, zl, x, core in itertools.product(*(range(n) for n in SIZES)):
        to_zh, *rest = move(zh, y, zl, x)
        pairs.append((device_of(zh, y, zl, x, core), device_of(to_zh ^ far, *rest, core)))
    return pairs


def to_column(zh, y, zl, x):
    block = zh * 8 + y
    return x >> 1, zl * 2 + (x & 1), block // 4, block % 4


def to_row(zh, y, zl, x):
    slot, block = y * 2 + zh, zl * 4 + x
    return block // 8, block % 8, slot % 4, slot // 4


def pack(values, scale):
    return (values.astype(jnp.float32) * scale).astype(jnp.float16)


def restore(values, scale):
    return (values.astype(jnp.float32) * (1.0 / scale)).astype(jnp.bfloat16)


def lookup(positions, energy_table):
    matches = positions[:, None] == jnp.arange(energy_table.shape[0], dtype=jnp.int32)[None, :]
    return jnp.sum(jnp.where(matches, energy_table[None, :], 0.0), axis=1)


def pair_gap(occupied_map, virtual_map, occupied_energy, virtual_energy, offset, length):
    occupied_part = lax.dynamic_slice_in_dim(occupied_map, offset, length, 0)
    virtual_part = lax.dynamic_slice_in_dim(virtual_map, offset, length, 0)
    return lookup(virtual_part, virtual_energy) - lookup(occupied_part, occupied_energy)


def contract(left, right):
    return lax.dot_general(
        left, right, (((0,), (0,)), ((), ())), preferred_element_type=jnp.float32
    )


def per_device(
    amplitudes, aux_left, aux_right, occupied_map, virtual_map, occupied_energy, virtual_energy
):
    rows, cols = amplitudes.shape
    core = lax.axis_index("core")
    row_block = lax.axis_index(ROW)
    col_block = lax.axis_index(COL + ("core",))

    pair = jnp.concatenate([aux_left.T, aux_right.T], axis=0)
    near = lax.all_gather(pair, ("zh", "core"), axis=0).reshape(2, 2, 128, cols)
    mine = lax.dynamic_index_in_dim(near, core, 1, keepdims=False)
    theirs = lax.dynamic_index_in_dim(near, 1 - core, 1, keepdims=False)
    left_near = jnp.concatenate(
        [
            lax.dynamic_slice_in_dim(mine, core * 32, 32, 1),
            lax.dynamic_slice_in_dim(theirs, core * 32, 32, 1),
        ],
        axis=1,
    )
    chunk = jnp.concatenate(
        [pack(left_near, LEFT_SCALE), pack(mine[:, 64:], RIGHT_SCALE)], axis=1
    )
    factors = lax.all_gather(chunk, "y", axis=0, tiled=True)
    factors = factors.reshape(2, 2, 2, 2, 128, cols)
    by_slot = factors.transpose(3, 2, 0, 1, 4, 5)
    left_kept = restore(by_slot[..., :32, :], LEFT_SCALE).reshape(512, cols)
    left_taken = restore(by_slot[..., 32:64, :], LEFT_SCALE).reshape(512, cols)
    right_cols = by_slot[..., 64:, :].reshape(4, 4, 2, 32, cols).transpose(0, 2, 1, 3, 4)
    right_cols = restore(right_cols, RIGHT_SCALE).reshape(1024, cols)
    other_amplitudes = lax.ppermute(amplitudes, "core", SWAP)

    partial = lax.dot_general(
        left_kept, amplitudes, (((1,), (1,)), ((), ())), preferred_element_type=jnp.float32
    ) + lax.dot_general(
        left_taken, other_amplitudes, (((1,), (1,)), ((), ())), preferred_element_type=jnp.float32
    )
    sent = (partial * SUM_SCALE).astype(jnp.float16).reshape(4, 128, rows)
    right_moved = lax.ppermute(pack(aux_right.T, RIGHT_SCALE), ALL, chips(to_row))
    arrived = lax.all_to_all(sent, "x", 0, 0)
    summed = jnp.sum(arrived.astype(jnp.float32), axis=0) * (LINE_SCALE / SUM_SCALE)
    sent = summed.astype(jnp.float16).reshape(4, 32, rows)
    arrived = lax.all_to_all(sent, "zl", 0, 0)
    arrived, right_moved = lax.optimization_barrier((arrived, right_moved))
    summed = jnp.sum(arrived.astype(jnp.float32), axis=0) * (1.0 / LINE_SCALE)
    rounded = lax.reduce_precision(summed, exponent_bits=8, mantissa_bits=7)
    fitted = rounded.astype(jnp.bfloat16)
    light = (rounded * FIT_SCALE).astype(jnp.float16)
    light = jnp.concatenate([light[:, :cols], light[:, cols:]], axis=0)

    same = lax.ppermute(fitted, ALL, chips(to_column))
    cross = lax.ppermute(fitted, ALL, chips(to_column, 1))
    both = lax.all_gather(jnp.concatenate([right_moved, light], axis=0), "zl", axis=0)
    both, same, cross = lax.optimization_barrier((both, same, cross))
    both = both.reshape(2, 2, 4, 32, cols)
    right_part = both[:, :, :2].transpose(0, 2, 1, 3, 4).reshape(256, cols)
    fitted_part = both[:, :, 2:].transpose(2, 0, 1, 3, 4).reshape(256, cols)
    both = jnp.concatenate([right_part, fitted_part], axis=0)
    low = lax.axis_index("zh") == 0
    below, above = jnp.where(low, same, cross), jnp.where(low, cross, same)
    mirror_chunk = jnp.stack(
        [below[:, :cols], above[:, :cols], below[:, cols:], above[:, cols:]]
    )
    mirror = jnp.broadcast_to(mirror_chunk[None], (8,) + mirror_chunk.shape)
    mirror = lax.all_to_all(mirror.reshape(16, 2, 32, cols), ("y", "core"), 0, 0)
    both = lax.all_gather(both, ("x", "core"), axis=0).reshape(4, 2, 512, cols)
    mirror = mirror.reshape(1024, cols)

    right_rows = jnp.concatenate(
        [restore(both[:, half, :256], RIGHT_SCALE).reshape(1024, cols) for half in range(2)], axis=1
    )
    fitted_rows = both[:, :, 256:].reshape(4, 2, 2, 128, cols)
    fitted_rows = jnp.concatenate(
        [restore(fitted_rows[:, :, half], FIT_SCALE).reshape(1024, cols) for half in range(2)], axis=1
    )
    total = contract(fitted_rows, right_cols) + contract(right_rows, mirror)
    row_gap = pair_gap(
        occupied_map, virtual_map, occupied_energy, virtual_energy, row_block * rows, rows
    )
    col_gap = pair_gap(
        occupied_map, virtual_map, occupied_energy, virtual_energy, col_block * cols, cols
    )
    return total / (row_gap[:, None] + col_gap[None, :])


def solution(mesh):
    fine = Mesh(mesh.devices.reshape(SIZES), ALL)
    by_block = P(ROW, COL + ("core",))
    by_aux = P(COL + ("core",), ROW)
    return jax.shard_map(
        per_device,
        mesh=fine,
        in_specs=(by_block, by_aux, by_aux, P(), P(), P(), P()),
        out_specs=by_block,
        check_vma=False,
    )
```

```python
import itertools

import jax
import jax.numpy as jnp
from jax import lax
from jax.sharding import Mesh
from jax.sharding import PartitionSpec as P

ROW = ("zh", "y")
COL = ("zl", "x")
ALL = ("zh", "y", "zl", "x", "core")
SIZES = (2, 8, 4, 4, 2)
SWAP = [(0, 1), (1, 0)]
LEFT_SCALE = 2.0**20
RIGHT_SCALE = 2.0**18
FIT_SCALE = 8.0
SUM_SCALE = 128.0
LINE_SCALE = 32.0


def device_of(zh, y, zl, x, core):
    return (((zh * 8 + y) * 4 + zl) * 4 + x) * 2 + core


def chips(move, far=0):
    pairs = []
    for zh, y, zl, x, core in itertools.product(*(range(n) for n in SIZES)):
        to_zh, *rest = move(zh, y, zl, x)
        pairs.append((device_of(zh, y, zl, x, core), device_of(to_zh ^ far, *rest, core)))
    return pairs


def to_column(zh, y, zl, x):
    block = zh * 8 + y
    return x >> 1, zl * 2 + (x & 1), block // 4, block % 4


def to_row(zh, y, zl, x):
    slot, block = y * 2 + zh, zl * 4 + x
    return block // 8, block % 8, slot % 4, slot // 4


def pack(values, scale):
    return (values.astype(jnp.float32) * scale).astype(jnp.float16)


def restore(values, scale):
    return (values.astype(jnp.float32) * (1.0 / scale)).astype(jnp.bfloat16)


def lookup(positions, energy_table):
    matches = positions[:, None] == jnp.arange(energy_table.shape[0], dtype=jnp.int32)[None, :]
    return jnp.sum(jnp.where(matches, energy_table[None, :], 0.0), axis=1)


def pair_gap(occupied_map, virtual_map, occupied_energy, virtual_energy, offset, length):
    occupied_part = lax.dynamic_slice_in_dim(occupied_map, offset, length, 0)
    virtual_part = lax.dynamic_slice_in_dim(virtual_map, offset, length, 0)
    return lookup(virtual_part, virtual_energy) - lookup(occupied_part, occupied_energy)


def contract(left, right):
    return lax.dot_general(
        left, right, (((0,), (0,)), ((), ())), preferred_element_type=jnp.float32
    )


def per_device(
    amplitudes, aux_left, aux_right, occupied_map, virtual_map, occupied_energy, virtual_energy
):
    rows, cols = amplitudes.shape
    core = lax.axis_index("core")
    row_block = lax.axis_index(ROW)
    col_block = lax.axis_index(COL + ("core",))

    near = lax.all_gather(aux_left.T, ("zh", "core"), axis=0).reshape(2, 2, 64, cols)
    mine = lax.dynamic_index_in_dim(near, core, 1, keepdims=False)
    theirs = lax.dynamic_index_in_dim(near, 1 - core, 1, keepdims=False)
    left_near = jnp.concatenate(
        [
            lax.dynamic_slice_in_dim(mine, core * 32, 32, 1),
            lax.dynamic_slice_in_dim(theirs, core * 32, 32, 1),
        ],
        axis=1,
    )
    chunk = jnp.concatenate(
        [
            pack(left_near, LEFT_SCALE).reshape(128, cols),
            pack(aux_right.T, RIGHT_SCALE),
        ],
        axis=0,
    )
    factors = lax.all_gather(chunk, "y", axis=0)
    by_slot = factors[:, :128].reshape(2, 2, 2, 2, 64, cols).transpose(3, 2, 0, 1, 4, 5)
    left_kept = restore(by_slot[..., :32, :], LEFT_SCALE).reshape(512, cols)
    left_taken = restore(by_slot[..., 32:64, :], LEFT_SCALE).reshape(512, cols)
    right_near = restore(factors[:, 128:], RIGHT_SCALE).reshape(512, cols)
    other_amplitudes = lax.ppermute(amplitudes, "core", SWAP)

    partial = lax.dot_general(
        left_kept, amplitudes, (((1,), (1,)), ((), ())), preferred_element_type=jnp.float32
    ) + lax.dot_general(
        left_taken, other_amplitudes, (((1,), (1,)), ((), ())), preferred_element_type=jnp.float32
    )
    sent = (partial * SUM_SCALE).astype(jnp.float16).reshape(4, 128, rows)
    right_moved = lax.ppermute(pack(aux_right.T, RIGHT_SCALE), ALL, chips(to_row))
    arrived = lax.all_to_all(sent, "x", 0, 0)
    low = lax.axis_index("zh") == 0
    summed = jnp.sum(arrived.astype(jnp.float32), axis=0) * (LINE_SCALE / SUM_SCALE)
    sent = summed.astype(jnp.float16).reshape(4, 32, rows)
    arrived = lax.all_to_all(sent, "zl", 0, 0)
    arrived, right_moved = lax.optimization_barrier((arrived, right_moved))
    summed = jnp.sum(arrived.astype(jnp.float32), axis=0) * (1.0 / LINE_SCALE)
    rounded = lax.reduce_precision(summed, exponent_bits=8, mantissa_bits=7)
    fitted = rounded.astype(jnp.bfloat16)
    light = (rounded * FIT_SCALE).astype(jnp.float16)
    light = jnp.concatenate([light[:, :cols], light[:, cols:]], axis=0)

    same = lax.ppermute(fitted, ALL, chips(to_column))
    cross = lax.ppermute(fitted, ALL, chips(to_column, 1))
    both = lax.all_gather(jnp.concatenate([right_moved, light], axis=0), "zl", axis=0)
    both, same, cross = lax.optimization_barrier((both, same, cross))
    both = both.reshape(2, 2, 4, 32, cols)
    right_part = both[:, :, :2].transpose(0, 2, 1, 3, 4).reshape(256, cols)
    fitted_part = both[:, :, 2:].transpose(2, 0, 1, 3, 4).reshape(256, cols)
    both = jnp.concatenate([right_part, fitted_part], axis=0)
    low = lax.axis_index("zh") == 0
    below, above = jnp.where(low, same, cross), jnp.where(low, cross, same)
    mirror_chunk = jnp.stack(
        [below[:, :cols], above[:, :cols], below[:, cols:], above[:, cols:]]
    )
    mirror = jnp.broadcast_to(mirror_chunk[None], (8,) + mirror_chunk.shape)
    mirror = lax.all_to_all(mirror.reshape(16, 2, 32, cols), ("y", "core"), 0, 0)
    right_far = lax.ppermute(right_near, "zh", SWAP)
    both = lax.all_gather(both, ("x", "core"), axis=0).reshape(4, 2, 512, cols)
    mirror = mirror.reshape(1024, cols)

    right_rows = jnp.concatenate(
        [restore(both[:, half, :256], RIGHT_SCALE).reshape(1024, cols) for half in range(2)], axis=1
    )
    fitted_rows = both[:, :, 256:].reshape(4, 2, 2, 128, cols)
    fitted_rows = jnp.concatenate(
        [restore(fitted_rows[:, :, half], FIT_SCALE).reshape(1024, cols) for half in range(2)], axis=1
    )
    right_cols = jnp.stack(
        [jnp.where(low, right_near, right_far), jnp.where(low, right_far, right_near)]
    )
    right_cols = right_cols.reshape(2, 2, 2, 2, 2, 32, cols).transpose(0, 3, 4, 1, 2, 5, 6)
    right_cols = right_cols.reshape(1024, cols)
    total = contract(fitted_rows, right_cols) + contract(right_rows, mirror)
    row_gap = pair_gap(
        occupied_map, virtual_map, occupied_energy, virtual_energy, row_block * rows, rows
    )
    col_gap = pair_gap(
        occupied_map, virtual_map, occupied_energy, virtual_energy, col_block * cols, cols
    )
    return total / (row_gap[:, None] + col_gap[None, :])


def solution(mesh):
    fine = Mesh(mesh.devices.reshape(SIZES), ALL)
    by_block = P(ROW, COL + ("core",))
    by_aux = P(COL + ("core",), ROW)
    return jax.shard_map(
        per_device,
        mesh=fine,
        in_specs=(by_block, by_aux, by_aux, P(), P(), P(), P()),
        out_specs=by_block,
        check_vma=False,
    )
```
